256 devices in a mesh: rows: 32 (over z, x), feat: 8 (over y, core).
Axes of the slice: x: 4, y: 4, z: 8, core: 2. Of those that a mesh axis runs over, the one named last changes fastest.
Arguments:
- points: float32 [8, 131072], P(None, 'rows'), may hold values from -4 to 4
- freq_index: int32 [8, 16384], P(None, 'feat'), may hold values from -12 to 12
- log_density: float32 [16384], P('feat'), may hold values from -3 to 2.7
- targets: float32 [131072], P('rows'), may hold values from -16 to 16
- probes: int32 [31, 131072], P(None, 'rows'), may hold values 0 or 1
Outputs:
- solution: float32 [32, 131072], P(None, 'rows')
- residual: float32 [32, 131072], P(None, 'rows')
The draws below stay inside these ranges and needn't reach their ends.
All inputs are finite; a program needn't handle non-finite values. No bound on the sum of `probes` on one device may be relied on, other than what follows from the above.
Results may differ from the reference program's by a relative error of at most 0.0025.
Values may be sent and summed in bfloat16 or wider, within the bound.
A program may use at most 128 MiB of HBM per device.

```python
import math
import jax
import jax.numpy as jnp
from jax import lax

DIM = 8
FREQS = 16384
PROBES = 31
ITERS = 2
NPTS = 131072


def draw_log_density(key, part):
    ramp = jnp.arange(FREQS, dtype=jnp.float32) / (FREQS - 1)
    base = jax.random.uniform(key, (FREQS,), jnp.float32, -2.5, 0.5)
    return base + math.log(3.0) * ramp


def draw_targets(key, part):
    ramp = jnp.arange(NPTS, dtype=jnp.float32) / (NPTS - 1)
    base = jnp.clip(jax.random.normal(key, (NPTS,), jnp.float32), -4.0, 4.0)
    return base * (1.0 + 2.0 * ramp)


def place_ends(array, rng, least, top_value):
    longest = array.shape.index(max(array.shape))
    spots = []
    for shift in (0, 1):
        where = [jax.random.randint(jax.random.fold_in(rng, axis), (), 0, length) for axis, length in enumerate(array.shape)]
        where[longest] = (where[longest] + shift) % array.shape[longest]
        spots.append(tuple(where))
    return array.at[spots[0]].set(least).at[spots[1]].set(top_value)


def steps_of(own_key, shape, pieces, smallest, high):
    loudness, own = 1.0, jax.random.fold_in(own_key, 6)
    for axis_at, parts in pieces:
        draws = jnp.exp(jax.random.uniform(jax.random.fold_in(own, axis_at), (parts,), jnp.float32, smallest / len(pieces), high / len(pieces)))
        loudness = loudness * jnp.repeat(draws, shape[axis_at] // parts).reshape([-1 if axis == axis_at else 1 for axis in range(len(shape))])
    return loudness


def gaussian(rng, extent, width, bound, pieces=(), kind=jnp.bfloat16):
    loudness = steps_of(rng, extent, pieces, -0.22, 0.18) if pieces else 1.0
    array = jax.random.normal(rng, extent, jnp.float32) * width * loudness
    return jnp.minimum(jnp.maximum(array, -bound), bound).astype(kind)


def setup_inputs(seed: int = 0) -> dict:
    splits = jax.random.split(jax.random.key(seed), 6)
    points = gaussian(splits[0], (DIM, NPTS), 0.7, 4.0, ((1, 32),), jnp.float32)
    freq_index = place_ends(jax.random.randint(splits[1], (DIM, FREQS), -12, 13), jax.random.fold_in(splits[1], 1), -12, 12).astype(jnp.int32)
    log_density = draw_log_density(jax.random.fold_in(splits[5], 71), 0)
    targets = draw_targets(jax.random.fold_in(splits[5], 71), 0)
    probes = place_ends((jax.random.randint(splits[4], (PROBES, NPTS), 0, 2) < 1).astype(jnp.int32), jax.random.fold_in(splits[4], 1), 0, 1)
    return {"points": points, "freq_index": freq_index, "log_density": log_density, "targets": targets, "probes": probes}


frequency_step = 0.25
noise_level = 1.0

def make_features(points, frequency, amplitude, first_row, block_rows):
    point_block = lax.dynamic_slice_in_dim(points, first_row, block_rows, 1)
    phases = jnp.dot(point_block.T, frequency, precision=lax.Precision.HIGHEST, preferred_element_type=jnp.float32)
    return jnp.concatenate([amplitude * jnp.cos(phases), amplitude * jnp.sin(phases)], axis=1).astype(jnp.bfloat16)

def project_down(direction_bf, points, frequency, amplitude, block_rows):
    blocks = points.shape[1] // block_rows
    feature_width = 2 * frequency.shape[1]

    def accumulate(block_index, running):
        first_row = (block_index * block_rows).astype(jnp.int32)
        feature_block = make_features(points, frequency, amplitude, first_row, block_rows)
        direction_block = lax.dynamic_slice_in_dim(direction_bf, first_row, block_rows, 1)
        return running + jnp.dot(direction_block, feature_block, preferred_element_type=jnp.float32)
    initial = jnp.zeros((direction_bf.shape[0], feature_width), jnp.float32)
    return lax.fori_loop(0, blocks, accumulate, initial)

def spread_up(coeff_bf, points, frequency, amplitude, block_rows):
    blocks = points.shape[1] // block_rows

    def place(block_index, images):
        first_row = (block_index * block_rows).astype(jnp.int32)
        feature_block = make_features(points, frequency, amplitude, first_row, block_rows)
        image_block = jnp.dot(coeff_bf, feature_block.T, preferred_element_type=jnp.float32)
        return lax.dynamic_update_slice_in_dim(images, image_block, first_row, 1)
    initial = jnp.zeros((coeff_bf.shape[0], points.shape[1]), jnp.float32)
    return lax.fori_loop(0, blocks, place, initial)

def reference(points, freq_index, log_density, targets, probes):
    frequency = frequency_step * freq_index.astype(jnp.float32)
    amplitude = jnp.exp(0.5 * log_density) / math.sqrt(FREQS)
    block_rows = math.gcd(NPTS, 1024)
    right_sides = jnp.concatenate([targets[None, :], (2 * probes - 1).astype(jnp.float32)], axis=0)
    solution = jnp.zeros_like(right_sides)
    residual = right_sides
    direction = right_sides
    residual_energy = lax.optimization_barrier(jnp.sum(residual * residual, axis=1))
    for iteration in range(ITERS):
        direction_bf = direction.astype(jnp.bfloat16)
        coeff_bf = project_down(direction_bf, points, frequency, amplitude, block_rows).astype(jnp.bfloat16)
        coeff_bf = lax.optimization_barrier(coeff_bf)
        images = spread_up(coeff_bf, points, frequency, amplitude, block_rows)
        coeff_wide = coeff_bf.astype(jnp.float32)
        curvature = lax.optimization_barrier(jnp.sum(coeff_wide * coeff_wide, axis=1)) + noise_level * lax.optimization_barrier(jnp.sum(direction * direction, axis=1))
        step_size = residual_energy / curvature
        solution = solution + step_size[:, None] * direction
        residual = residual - step_size[:, None] * (images + noise_level * direction)
        if iteration + 1 < ITERS:
            energy_next = lax.optimization_barrier(jnp.sum(residual * residual, axis=1))
            mixing = energy_next / residual_energy
            direction = residual + mixing[:, None] * direction
            residual_energy = energy_next
    return (solution, residual)
```

```python
import functools
import math

import jax
import jax.numpy as jnp
from jax import lax
from jax.experimental import pallas as pl
from jax.experimental.pallas import tpu as pltpu
from jax.sharding import PartitionSpec as P

FREQS = 16384
LANES = 128
TURN = 0.25 / (2.0 * math.pi)
SIN_TERMS = (4.44286798219978, -7.307445410802044, 3.594802081647382, -0.7844035671777289)
COS_TERMS = (
    1.4142134965673496,
    -6.9788509883336225,
    5.739461171609176,
    -1.8835629899096435,
    0.310698192272404,
)
F32 = jnp.float32
BF16 = jnp.bfloat16
MESH = pl.DeviceIdType.MESH


def scaled_trig(turns, amplitude):
    r = turns - jnp.round(turns)
    u = r * r
    half_sin = SIN_TERMS[-1]
    for term in SIN_TERMS[-2::-1]:
        half_sin = half_sin * u + term
    half_sin = half_sin * r
    half_cos = COS_TERMS[-1]
    for term in COS_TERMS[-2::-1]:
        half_cos = half_cos * u + term
    scaled = amplitude * half_sin
    return amplitude - scaled * half_sin, scaled * half_cos


def three_way(value):
    high = value.astype(BF16).astype(F32)
    middle = (value - high).astype(BF16).astype(F32)
    return high, middle, value - high - middle


def spread(value, axis, shape):
    high, middle, low = three_way(value)
    place = lax.broadcasted_iota(jnp.int32, shape, axis)
    high, middle, low = (jnp.broadcast_to(part, shape) for part in (high, middle, low))
    zero = jnp.zeros(shape, F32)
    return jnp.where(
        place == 0, high, jnp.where(place == 1, middle, jnp.where(place == 2, low, zero))
    )


def lane_fold(value):
    total = value[:, :LANES]
    for start in range(LANES, value.shape[1], LANES):
        total = total + value[:, start : start + LANES]
    return total


def rows_to_lanes(parts):
    stacked = jnp.concatenate(parts, axis=0)
    rest = LANES - stacked.shape[0]
    stacked = jnp.concatenate([stacked, jnp.zeros((rest, LANES), F32)], axis=0)
    return jnp.sum(stacked.T, axis=0, keepdims=True)


def lanes_to_rows(row, offset, count):
    shape = (count, LANES)
    here = lax.broadcasted_iota(jnp.int32, shape, 0) + offset
    lane = lax.broadcasted_iota(jnp.int32, shape, 1)
    picked = jnp.where(here == lane, jnp.broadcast_to(row, shape), jnp.zeros(shape, F32))
    return jnp.sum(picked, axis=1, keepdims=True)


def kernel(
    sizes, points, freq, density, targets, probes, x_out, r_out,
    table, turns_t, rhs, rhs_bf,
    c_part, c_send, c_recv, c_own, c_all, s_send, s_recv, d_all,
    i_part, i_send, i_recv, i_all, j_send, j_recv, j_all,
    a_src, b_src, c_src, d_src, send_sem, recv_sem,
):
    rows, feats = sizes
    me_r = lax.axis_index("rows")
    me_f = lax.axis_index("feat")
    here = points.shape[1]
    width = freq.shape[1]
    sides = rhs.shape[0]
    share = here // feats
    batch_r = min(512, here)
    batch_f = min(256, width)

    barrier = pltpu.get_barrier_semaphore()

    def greet_row(step, carry):
        pl.semaphore_signal(
            barrier, inc=1, device_id=(lax.rem(me_r + step, rows), me_f), device_id_type=MESH
        )
        return carry

    def greet_feat(step, carry):
        pl.semaphore_signal(
            barrier, inc=1, device_id=(me_r, lax.rem(me_f + step, feats)), device_id_type=MESH
        )
        return carry

    lax.fori_loop(1, rows, greet_row, 0)
    lax.fori_loop(1, feats, greet_feat, 0)

    def to_row(phase, src, dst, step):
        return pltpu.make_async_remote_copy(
            src_ref=src, dst_ref=dst, send_sem=send_sem.at[phase], recv_sem=recv_sem.at[phase],
            device_id=(lax.rem(me_r + step, rows), me_f), device_id_type=MESH,
        )

    def to_feat(phase, src, dst, step):
        return pltpu.make_async_remote_copy(
            src_ref=src, dst_ref=dst, send_sem=send_sem.at[phase], recv_sem=recv_sem.at[phase],
            device_id=(me_r, lax.rem(me_f + step, feats)), device_id_type=MESH,
        )

    def await_bytes(sem, ref):
        pltpu.make_async_copy(ref, ref, sem).wait()

    rhs[0:1, :] = targets[...]
    rhs[1:sides, :] = (2 * probes[...] - 1).astype(F32)
    right = rhs[...]
    rhs_bf[...] = right.astype(BF16)
    scaled = points[...] * TURN
    high, middle, low = three_way(scaled)
    stacked = jnp.concatenate([high, middle, low, jnp.zeros_like(high)], axis=0)
    turns_t[...] = stacked.T.astype(BF16)
    tail = spread(rows_to_lanes([lane_fold(right * right)]), 0, (16, LANES)).astype(BF16)

    def set_tail(buffer, tail):
        def put(chunk, carry):
            buffer[chunk, sides : sides + 16, :] = tail
            return carry

        lax.fori_loop(0, rows, put, 0)

    set_tail(c_send, tail)
    pl.semaphore_wait(barrier, rows + feats - 2)

    def ship(phase, buffer, landing, chunk, value, keep):
        buffer[chunk, 0:sides, :] = value.astype(BF16)
        step = lax.rem(chunk + rows - me_r, rows)

        @pl.when(chunk == me_r)
        def _():
            keep[...] = value

        @pl.when(chunk != me_r)
        def _():
            to_row(phase, buffer.at[chunk], landing.at[step - 1], step).start()

    blocks_f = width // batch_f
    per_block = batch_f // LANES
    half = rows // 2
    own_block = lax.rem(me_r, half) // per_block

    def make_block(index, carry):
        block = lax.rem(index + own_block + 1, blocks_f)
        at = pl.multiple_of(block * batch_f, batch_f)
        whole = freq[:, pl.ds(at, batch_f)].astype(F32)
        whole = jnp.concatenate([whole, whole, whole, jnp.zeros_like(whole)], axis=0).astype(BF16)
        strength = jnp.exp(0.5 * density[:, pl.ds(at, batch_f)]) * (1.0 / math.sqrt(FREQS))

        def fill(step, carry):
            first = pl.multiple_of(step * batch_r, batch_r)
            turns = jnp.dot(
                turns_t[pl.ds(first, batch_r), :], whole, preferred_element_type=F32
            )
            cosine, sine = scaled_trig(turns, strength)
            table[pl.ds(first, batch_r), pl.ds(at, batch_f)] = cosine.astype(BF16)
            table[pl.ds(first, batch_r), pl.ds(width + at, batch_f)] = sine.astype(BF16)
            return carry

        lax.fori_loop(0, here // batch_r, fill, 0)
        for part in range(2):
            sums = jnp.dot(
                rhs_bf[...],
                table[:, pl.ds(part * width + at, batch_f)],
                preferred_element_type=F32,
            )
            for piece in range(per_block):
                chunk = part * half + block * per_block + piece
                ship(0, c_send, c_recv, chunk, sums[:, piece * LANES : (piece + 1) * LANES], c_part)
        return carry

    lax.fori_loop(0, blocks_f, make_block, 0)

    def collect_rows(phase, landing, buffer, own):
        await_bytes(recv_sem.at[phase], landing)

        def add(slot, carry):
            total, extra = carry
            total = total + landing[slot, 0:sides, :].astype(F32)
            return total, extra + landing[slot, sides : sides + 16, :].astype(F32)

        first = (own[...], buffer[0, sides : sides + 16, :].astype(F32))
        total, extra = lax.fori_loop(0, rows - 1, add, first)
        return total, jnp.sum(extra, axis=0, keepdims=True)

    def share_rows(phase, source, everyone, value):
        source[...] = value
        everyone[me_r] = value

        def send(step, carry):
            to_row(phase, source, everyone.at[me_r], step).start()
            return carry

        lax.fori_loop(1, rows, send, 0)
        await_bytes(recv_sem.at[phase], everyone.at[pl.ds(0, rows - 1)])

    total, extra = collect_rows(0, c_recv, c_send, c_part)
    energy = lanes_to_rows(extra, 0, sides)
    c_own[...] = total
    share_rows(1, a_src, c_all, total.astype(BF16))

    def spread_up(phase, everyone, buffer, landing, own):
        wide = everyone_cat(everyone).astype(F32)
        squares = jnp.sum(lane_fold(wide * wide), axis=1, keepdims=True)
        tail = jnp.where(
            lax.broadcasted_iota(jnp.int32, (sides, LANES), 1) == 0,
            jnp.broadcast_to(squares, (sides, LANES)),
            jnp.zeros((sides, LANES), F32),
        )

        def one(index, carry):
            step = index + 1
            target = lax.rem(me_f + step, feats)
            at = pl.multiple_of(target * share, share)
            images = lax.dot_general(
                everyone_cat(everyone), table[pl.ds(at, share), :],
                (((1,), (1,)), ((), ())), preferred_element_type=F32,
            )
            buffer[target, :, 0:share] = images
            buffer[target, :, share : share + LANES] = tail

            @pl.when(step < feats)
            def _():
                to_feat(phase, buffer.at[target], landing.at[step - 1], step).start()

            @pl.when(step == feats)
            def _():
                own[...] = images

            return carry

        lax.fori_loop(0, feats, one, 0)
        await_bytes(recv_sem.at[phase], landing)
        total = own[...]
        extra = tail
        for slot in range(feats - 1):
            total = total + landing[slot, :, 0:share]
            extra = extra + landing[slot, :, share : share + LANES]
        return total, jnp.sum(extra, axis=1, keepdims=True)

    def everyone_cat(everyone):
        return jnp.concatenate([everyone[chunk] for chunk in range(rows)], axis=1)

    def share_feats(phase, source, everyone, value):
        source[...] = value
        everyone[me_f] = value

        def send(step, carry):
            to_feat(phase, source, everyone.at[me_f], step).start()
            return carry

        lax.fori_loop(1, feats, send, 0)
        await_bytes(recv_sem.at[phase], everyone.at[pl.ds(0, feats - 1)])

    total, squares = spread_up(2, c_all, i_send, i_recv, i_part)
    alpha0 = energy / (squares + energy)
    share_feats(3, b_src, i_all, total)

    def images_of(everyone):
        return jnp.concatenate([everyone[part] for part in range(feats)], axis=1)

    images = images_of(i_all)
    rhs_bf[...] = images.astype(BF16)
    residual = (1.0 - alpha0) * rhs[...] - alpha0 * images
    cross = lane_fold(residual * rhs[...])
    tail = spread(rows_to_lanes([lane_fold(residual * residual), cross]), 0, (16, LANES))
    set_tail(s_send, tail.astype(BF16))

    group = min(4, rows)
    blocks_d = rows // group
    own_group = me_r // group

    def project(index, carry):
        block = lax.rem(index + own_group + 1, blocks_d)
        at = pl.multiple_of(block * (group * LANES), group * LANES)
        sums = jnp.dot(
            rhs_bf[...], table[:, pl.ds(at, group * LANES)], preferred_element_type=F32
        )
        for piece in range(group):
            chunk = block * group + piece
            ship(4, s_send, s_recv, chunk, sums[:, piece * LANES : (piece + 1) * LANES], c_part)
        return carry

    lax.fori_loop(0, blocks_d, project, 0)
    total, extra = collect_rows(4, s_recv, s_send, c_part)
    energy_next = lanes_to_rows(extra, 0, sides)
    cross = lanes_to_rows(extra, sides, sides)
    beta = energy_next / energy
    total = (1.0 - alpha0 + beta) * c_own[...] - alpha0 * total
    share_rows(5, c_src, d_all, total.astype(BF16))

    total, squares = spread_up(6, d_all, j_send, j_recv, i_part)
    direction_energy = energy_next + beta * (2.0 * cross + beta * energy)
    alpha1 = energy_next / (squares + direction_energy)
    share_feats(7, d_src, j_all, total)

    right = rhs[...]
    first_images = images_of(i_all)
    second_images = images_of(j_all)
    residual = (1.0 - alpha0) * right - alpha0 * first_images
    direction = residual + beta * right
    x_out[...] = alpha0 * right + alpha1 * direction
    r_out[...] = residual - alpha1 * (second_images + direction)

    for phase, ref in (
        (0, c_send.at[pl.ds(0, rows - 1)]), (1, c_all.at[pl.ds(0, rows - 1)]),
        (2, i_send.at[pl.ds(0, feats - 1)]), (3, i_all.at[pl.ds(0, feats - 1)]),
        (4, s_send.at[pl.ds(0, rows - 1)]), (5, d_all.at[pl.ds(0, rows - 1)]),
        (6, j_send.at[pl.ds(0, feats - 1)]), (7, j_all.at[pl.ds(0, feats - 1)]),
    ):
        await_bytes(send_sem.at[phase], ref)


def local(sizes, points, freq_index, log_density, targets, probes):
    rows, feats = sizes
    here = points.shape[1]
    width = freq_index.shape[1]
    sides = probes.shape[0] + 1
    share = here // feats
    vmem = pl.BlockSpec(memory_space=pltpu.VMEM)
    out = jax.ShapeDtypeStruct((sides, here), F32)
    block = (sides + 16, LANES)
    wide = (sides, share + LANES)
    scratch = [
        pltpu.VMEM((here, 2 * width), BF16),
        pltpu.VMEM((here, 32), BF16),
        pltpu.VMEM((sides, here), F32),
        pltpu.VMEM((sides, here), BF16),
        pltpu.VMEM((sides, LANES), F32),
        pltpu.VMEM((rows, *block), BF16),
        pltpu.VMEM((rows - 1, *block), BF16),
        pltpu.VMEM((sides, LANES), F32),
        pltpu.VMEM((rows, sides, LANES), BF16),
        pltpu.VMEM((rows, *block), BF16),
        pltpu.VMEM((rows - 1, *block), BF16),
        pltpu.VMEM((rows, sides, LANES), BF16),
        pltpu.VMEM((sides, share), F32),
        pltpu.VMEM((feats, *wide), F32),
        pltpu.VMEM((feats - 1, *wide), F32),
        pltpu.VMEM((feats, sides, share), F32),
        pltpu.VMEM((feats, *wide), F32),
        pltpu.VMEM((feats - 1, *wide), F32),
        pltpu.VMEM((feats, sides, share), F32),
        pltpu.VMEM((sides, LANES), BF16),
        pltpu.VMEM((sides, share), F32),
        pltpu.VMEM((sides, LANES), BF16),
        pltpu.VMEM((sides, share), F32),
        pltpu.SemaphoreType.DMA((8,)),
        pltpu.SemaphoreType.DMA((8,)),
    ]
    return pl.pallas_call(
        functools.partial(kernel, sizes),
        out_shape=(out, out),
        in_specs=[vmem] * 5,
        out_specs=(vmem, vmem),
        scratch_shapes=scratch,
        name="regress",
        compiler_params=pltpu.CompilerParams(
            collective_id=0, has_side_effects=True, vmem_limit_bytes=56 << 20
        ),
    )(points, freq_index, log_density.reshape(1, width), targets.reshape(1, here), probes)


def solution(mesh):
    sizes = (mesh.shape["rows"], mesh.shape["feat"])
    in_specs = (P(None, "rows"), P(None, "feat"), P("feat"), P("rows"), P(None, "rows"))
    out_specs = (P(None, "rows"), P(None, "rows"))
    return jax.shard_map(
        functools.partial(local, sizes),
        mesh=mesh, in_specs=in_specs, out_specs=out_specs, check_vma=False,
    )
```

```python
import functools
import math

import jax
import jax.numpy as jnp
from jax import lax
from jax.experimental import pallas as pl
from jax.experimental.pallas import tpu as pltpu
from jax.sharding import PartitionSpec as P

FREQS = 16384
LANES = 128
TURN = 0.25 / (2.0 * math.pi)
SIN_TERMS = (4.44286798219978, -7.307445410802044, 3.594802081647382, -0.7844035671777289)
COS_TERMS = (1.414204080722155, -6.977642062283957, 5.715238417642065, -1.728348665863172)
F32 = jnp.float32
BF16 = jnp.bfloat16
MESH = pl.DeviceIdType.MESH


def scaled_trig(turns, amplitude):
    r = turns - jnp.round(turns)
    u = r * r
    half_sin = SIN_TERMS[-1]
    for term in SIN_TERMS[-2::-1]:
        half_sin = half_sin * u + term
    half_sin = half_sin * r
    half_cos = COS_TERMS[-1]
    for term in COS_TERMS[-2::-1]:
        half_cos = half_cos * u + term
    scaled = amplitude * half_sin
    return amplitude - scaled * half_sin, scaled * half_cos


def three_way(value):
    high = value.astype(BF16).astype(F32)
    middle = (value - high).astype(BF16).astype(F32)
    return high, middle, value - high - middle


def spread(value, axis, shape):
    high, middle, low = three_way(value)
    place = lax.broadcasted_iota(jnp.int32, shape, axis)
    high, middle, low = (jnp.broadcast_to(part, shape) for part in (high, middle, low))
    zero = jnp.zeros(shape, F32)
    return jnp.where(
        place == 0, high, jnp.where(place == 1, middle, jnp.where(place == 2, low, zero))
    )


def lane_fold(value):
    total = value[:, :LANES]
    for start in range(LANES, value.shape[1], LANES):
        total = total + value[:, start : start + LANES]
    return total


def rows_to_lanes(parts):
    stacked = jnp.concatenate(parts, axis=0)
    rest = LANES - stacked.shape[0]
    stacked = jnp.concatenate([stacked, jnp.zeros((rest, LANES), F32)], axis=0)
    return jnp.sum(stacked.T, axis=0, keepdims=True)


def lanes_to_rows(row, offset, count):
    shape = (count, LANES)
    here = lax.broadcasted_iota(jnp.int32, shape, 0) + offset
    lane = lax.broadcasted_iota(jnp.int32, shape, 1)
    picked = jnp.where(here == lane, jnp.broadcast_to(row, shape), jnp.zeros(shape, F32))
    return jnp.sum(picked, axis=1, keepdims=True)


def kernel(
    sizes, points, freq, density, targets, probes, x_out, r_out,
    table, turns_t, rhs, lhs, acc,
    c_part, c_send, c_recv, c_own, c_all, s_send, s_recv, d_all,
    i_part, i_own, i_send, i_recv, i_all, j_send, j_recv, j_all, g_all, h_all,
    a_src, b_src, c_src, d_src, e_src, f_src, send_sem, recv_sem, gather_sem,
):
    rows, feats = sizes
    me_r = lax.axis_index("rows")
    me_f = lax.axis_index("feat")
    here = points.shape[1]
    width = freq.shape[1]
    sides = rhs.shape[0]
    share = here // feats
    blocks = block_count(rows)
    members = rows // blocks
    span = width // blocks
    batch = min(1024, here)
    my_block = lax.rem(me_r, blocks)
    my_place = my_block * members + me_r // blocks

    barrier = pltpu.get_barrier_semaphore()

    def greet_row(step, carry):
        pl.semaphore_signal(
            barrier, inc=1, device_id=(lax.rem(me_r + step, rows), me_f), device_id_type=MESH
        )
        return carry

    def greet_feat(step, carry):
        pl.semaphore_signal(
            barrier, inc=1, device_id=(me_r, lax.rem(me_f + step, feats)), device_id_type=MESH
        )
        return carry

    lax.fori_loop(1, rows, greet_row, 0)
    lax.fori_loop(1, feats, greet_feat, 0)

    def to_row(phase, arrival, src, dst, step):
        return pltpu.make_async_remote_copy(
            src_ref=src, dst_ref=dst, send_sem=send_sem.at[phase], recv_sem=arrival,
            device_id=(lax.rem(me_r + step, rows), me_f), device_id_type=MESH,
        )

    def to_feat(phase, src, dst, step):
        return pltpu.make_async_remote_copy(
            src_ref=src, dst_ref=dst, send_sem=send_sem.at[phase], recv_sem=recv_sem.at[phase],
            device_id=(me_r, lax.rem(me_f + step, feats)), device_id_type=MESH,
        )

    def await_bytes(sem, ref):
        pltpu.make_async_copy(ref, ref, sem).wait()

    rhs[0:1, :] = targets[...]
    rhs[1:sides, :] = (2 * probes[...] - 1).astype(F32)
    right = rhs[...]
    lhs[...] = right.astype(BF16)
    high, middle, low = three_way(points[...] * TURN)
    stacked = jnp.concatenate([high, middle, low, jnp.zeros_like(high)], axis=0)
    turns_t[...] = stacked.T.astype(BF16)
    tail = spread(rows_to_lanes([lane_fold(right * right)]), 0, (16, LANES)).astype(BF16)

    def set_tail(buffer, tail):
        def put(chunk, carry):
            buffer[chunk, sides : sides + 16, :] = tail
            return carry

        lax.fori_loop(0, rows, put, 0)

    set_tail(c_send, tail)

    def make_block(block):
        at = block * span
        whole = freq[:, at : at + span].astype(F32)
        whole = jnp.concatenate([whole, whole, whole, jnp.zeros_like(whole)], axis=0).astype(BF16)
        strength = jnp.exp(0.5 * density[:, at : at + span]) * (1.0 / math.sqrt(FREQS))

        def fill(step, carry):
            first = pl.multiple_of(step * batch, batch)
            turns = jnp.dot(turns_t[pl.ds(first, batch), :], whole, preferred_element_type=F32)
            cosine, sine = scaled_trig(turns, strength)
            table[pl.ds(first, batch), 2 * at : 2 * at + span] = cosine.astype(BF16)
            table[pl.ds(first, batch), 2 * at + span : 2 * (at + span)] = sine.astype(BF16)
            return carry

        lax.fori_loop(0, here // batch, fill, 0)

    def project(block, buffer):
        for part in range(2):
            at = (2 * block + part) * span
            sums = jnp.dot(lhs[...], table[:, at : at + span], preferred_element_type=F32)
            for piece in range(span // LANES):
                member = part * (members // 2) + piece
                value = sums[:, piece * LANES : (piece + 1) * LANES]
                buffer[block * members + member, 0:sides, :] = value.astype(BF16)

                @pl.when(me_r == member * blocks + block)
                def _():
                    c_part[...] = value

    def ship(phase, block, buffer, landing):
        def send(member, carry):
            step = lax.rem(member * blocks + block + rows - me_r, rows)

            @pl.when(step != 0)
            def _():
                to_row(
                    phase, recv_sem.at[phase], buffer.at[block * members + member],
                    landing.at[step - 1], step,
                ).start()

            return carry

        lax.fori_loop(0, members, send, 0)

    def collect(phase, landing, buffer):
        await_bytes(recv_sem.at[phase], landing)

        def add(slot, carry):
            total, extra = carry
            total = total + landing[slot, 0:sides, :].astype(F32)
            return total, extra + landing[slot, sides : sides + 16, :].astype(F32)

        first = (c_part[...], buffer[0, sides : sides + 16, :].astype(F32))
        total, extra = lax.fori_loop(0, rows - 1, add, first)
        return total, jnp.sum(extra, axis=0, keepdims=True)

    def share_rows(phase, block, source, everyone, value):
        source[...] = value
        everyone[my_place] = value

        def send(step, carry):
            arrival = gather_sem.at[phase // 4, block]
            to_row(phase, arrival, source, everyone.at[my_place], step).start()
            return carry

        lax.fori_loop(1, rows, send, 0)

    def await_block(phase, block, everyone):
        arrival = gather_sem.at[phase // 4, block]

        @pl.when(my_block == block)
        def _():
            await_bytes(arrival, everyone.at[pl.ds(block * members, members - 1)])

        @pl.when(my_block != block)
        def _():
            await_bytes(arrival, everyone.at[pl.ds(block * members, members)])

    def gathered(everyone, first, last):
        places = range(first * members, last * members)
        return jnp.concatenate([everyone[place] for place in places], axis=1)

    def raise_block(block, everyone):
        left = gathered(everyone, block, block + 1)

        def one(step, carry):
            at = pl.multiple_of(step * batch, batch)
            part = lax.dot_general(
                left, table[pl.ds(at, batch), 2 * block * span : 2 * (block + 1) * span],
                (((1,), (1,)), ((), ())), preferred_element_type=F32,
            )
            acc[:, pl.ds(at, batch)] = part if block == 0 else acc[:, pl.ds(at, batch)] + part
            return carry

        lax.fori_loop(0, here // batch, one, 0)

    def raise_rest(phase, early, everyone, buffer, landing, norms, norm_src):
        wide = gathered(everyone, 0, blocks).astype(F32)
        norm_src[...] = jnp.broadcast_to(rows_to_lanes([lane_fold(wide * wide)]), (8, LANES))
        norms[me_f] = norm_src[...]

        def send(step, carry):
            to_feat(phase + 6, norm_src, norms.at[me_f], step).start()
            return carry

        lax.fori_loop(1, feats, send, 0)

        def one(index, carry):
            step = index + 1
            target = lax.rem(me_f + step, feats)
            at = pl.multiple_of(target * share, share)
            images = acc[:, pl.ds(at, share)] + lax.dot_general(
                gathered(everyone, early, blocks),
                table[pl.ds(at, share), 2 * early * span : 2 * width],
                (((1,), (1,)), ((), ())), preferred_element_type=F32,
            )
            buffer[target] = images

            @pl.when(step < feats)
            def _():
                to_feat(phase, buffer.at[target], landing.at[step - 1], step).start()

            @pl.when(step == feats)
            def _():
                i_part[...] = images

            return carry

        lax.fori_loop(0, feats, one, 0)
        await_bytes(recv_sem.at[phase + 6], norms.at[pl.ds(0, feats - 1)])
        squares = norms[0, 0:1, :]
        for part in range(1, feats):
            squares = squares + norms[part, 0:1, :]
        await_bytes(recv_sem.at[phase], landing)
        total = i_part[...]
        for slot in range(feats - 1):
            total = total + landing[slot]
        return total, lanes_to_rows(squares, 0, sides)

    def share_feats(phase, source, everyone, value):
        source[...] = value
        everyone[me_f] = value

        def send(step, carry):
            to_feat(phase, source, everyone.at[me_f], step).start()
            return carry

        lax.fori_loop(1, feats, send, 0)

    def await_feats(phase, everyone):
        await_bytes(recv_sem.at[phase], everyone.at[pl.ds(0, feats - 1)])
        return jnp.concatenate([everyone[part] for part in range(feats)], axis=1)

    early = max(1, blocks - 2)

    def own_first(block):
        @pl.when(my_block == block)
        def _():
            total, extra = collect(0, c_recv, c_send)
            c_own[0:sides, :] = total
            c_own[sides : sides + 8, :] = jnp.broadcast_to(extra, (8, LANES))
            share_rows(1, block, a_src, c_all, total.astype(BF16))

    make_block(0)
    project(0, c_send)
    make_block(1)
    pl.semaphore_wait(barrier, rows + feats - 2)
    ship(0, 0, c_send, c_recv)
    project(1, c_send)
    ship(0, 1, c_send, c_recv)
    for block in range(2, blocks):
        make_block(block)
        project(block, c_send)
        ship(0, block, c_send, c_recv)
        own_first(block - 2)
    own_first(blocks - 2)
    for block in range(early):
        await_block(0, block, c_all)
        raise_block(block, c_all)
        if block == 0:
            own_first(blocks - 1)
    for block in range(early, blocks):
        await_block(0, block, c_all)
    total, squares = raise_rest(2, early, c_all, i_send, i_recv, g_all, e_src)
    i_own[...] = total
    share_feats(3, b_src, i_all, total.astype(BF16))
    energy = lanes_to_rows(c_own[sides : sides + 1, :], 0, sides)
    alpha0 = energy / (squares + energy)
    images = await_feats(3, i_all)
    lhs[...] = images
    residual = (1.0 - alpha0) * rhs[...] - alpha0 * images.astype(F32)
    tail = rows_to_lanes([lane_fold(residual * residual), lane_fold(residual * rhs[...])])
    set_tail(s_send, spread(tail, 0, (16, LANES)).astype(BF16))

    def own_second(block):
        @pl.when(my_block == block)
        def _():
            total, extra = collect(4, s_recv, s_send)
            beta = lanes_to_rows(extra, 0, sides) / energy
            total = (1.0 - alpha0 + beta) * c_own[0:sides, :] - alpha0 * total
            c_own[sides : sides + 8, :] = jnp.broadcast_to(extra, (8, LANES))
            share_rows(5, block, c_src, d_all, total.astype(BF16))

    for block in range(blocks):
        project(block, s_send)
        ship(4, block, s_send, s_recv)
        if block >= 2:
            own_second(block - 2)
    if blocks == 2:
        own_second(0)
    for block in range(early):
        await_block(4, block, d_all)
        raise_block(block, d_all)
        if block == 0:
            for late in range(early, blocks):
                own_second(late)
    for block in range(early, blocks):
        await_block(4, block, d_all)
    total, squares = raise_rest(6, early, d_all, j_send, j_recv, h_all, f_src)
    energy_next = lanes_to_rows(c_own[sides : sides + 1, :], 0, sides)
    cross = lanes_to_rows(c_own[sides : sides + 1, :], sides, sides)
    beta = energy_next / energy
    direction_energy = energy_next + beta * (2.0 * cross + beta * energy)
    alpha1 = energy_next / (squares + direction_energy)

    mine = rhs[:, pl.ds(pl.multiple_of(me_f * share, share), share)]
    residual = (1.0 - alpha0) * mine - alpha0 * i_own[...]
    residual = residual - alpha1 * (total + residual + beta * mine)
    share_feats(7, d_src, j_all, residual.astype(BF16))
    right = rhs[...]
    residual = (1.0 - alpha0) * right - alpha0 * lhs[...].astype(F32)
    x_out[...] = alpha0 * right + alpha1 * (residual + beta * right)
    r_out[...] = await_feats(7, j_all).astype(F32)

    for phase, ref in (
        (0, c_recv), (1, c_all.at[pl.ds(0, rows - 1)]),
        (2, i_recv), (3, i_all.at[pl.ds(0, feats - 1)]),
        (4, s_recv), (5, d_all.at[pl.ds(0, rows - 1)]),
        (6, j_recv), (7, j_all.at[pl.ds(0, feats - 1)]),
        (8, g_all.at[pl.ds(0, feats - 1)]), (12, h_all.at[pl.ds(0, feats - 1)]),
    ):
        await_bytes(send_sem.at[phase], ref)


def block_count(rows):
    return 4 if rows % 8 == 0 else 2


def local(sizes, points, freq_index, log_density, targets, probes):
    rows, feats = sizes
    here = points.shape[1]
    width = freq_index.shape[1]
    sides = probes.shape[0] + 1
    share = here // feats
    vmem = pl.BlockSpec(memory_space=pltpu.VMEM)
    out = jax.ShapeDtypeStruct((sides, here), F32)
    block = (sides + 16, LANES)
    scratch = [
        pltpu.VMEM((here, 2 * width), BF16),
        pltpu.VMEM((here, 32), BF16),
        pltpu.VMEM((sides, here), F32),
        pltpu.VMEM((sides, here), BF16),
        pltpu.VMEM((sides, here), F32),
        pltpu.VMEM((sides, LANES), F32),
        pltpu.VMEM((rows, *block), BF16),
        pltpu.VMEM((rows - 1, *block), BF16),
        pltpu.VMEM((sides + 8, LANES), F32),
        pltpu.VMEM((rows, sides, LANES), BF16),
        pltpu.VMEM((rows, *block), BF16),
        pltpu.VMEM((rows - 1, *block), BF16),
        pltpu.VMEM((rows, sides, LANES), BF16),
        pltpu.VMEM((sides, share), F32),
        pltpu.VMEM((sides, share), F32),
        pltpu.VMEM((feats, sides, share), F32),
        pltpu.VMEM((feats - 1, sides, share), F32),
        pltpu.VMEM((feats, sides, share), BF16),
        pltpu.VMEM((feats, sides, share), F32),
        pltpu.VMEM((feats - 1, sides, share), F32),
        pltpu.VMEM((feats, sides, share), BF16),
        pltpu.VMEM((feats, 8, LANES), F32),
        pltpu.VMEM((feats, 8, LANES), F32),
        pltpu.VMEM((sides, LANES), BF16),
        pltpu.VMEM((sides, share), BF16),
        pltpu.VMEM((sides, LANES), BF16),
        pltpu.VMEM((sides, share), BF16),
        pltpu.VMEM((8, LANES), F32),
        pltpu.VMEM((8, LANES), F32),
        pltpu.SemaphoreType.DMA((13,)),
        pltpu.SemaphoreType.DMA((13,)),
        pltpu.SemaphoreType.DMA((2, block_count(rows))),
    ]
    return pl.pallas_call(
        functools.partial(kernel, sizes),
        out_shape=(out, out),
        in_specs=[vmem] * 5,
        out_specs=(vmem, vmem),
        scratch_shapes=scratch,
        name="regress",
        compiler_params=pltpu.CompilerParams(
            collective_id=0, has_side_effects=True, vmem_limit_bytes=56 << 20
        ),
    )(points, freq_index, log_density.reshape(1, width), targets.reshape(1, here), probes)


def solution(mesh):
    sizes = (mesh.shape["rows"], mesh.shape["feat"])
    in_specs = (P(None, "rows"), P(None, "feat"), P("feat"), P("rows"), P(None, "rows"))
    out_specs = (P(None, "rows"), P(None, "rows"))
    return jax.shard_map(
        functools.partial(local, sizes),
        mesh=mesh, in_specs=in_specs, out_specs=out_specs, check_vma=False,
    )
```

```python
import functools
import math
from types import SimpleNamespace

import jax
import jax.numpy as jnp
from jax import lax
from jax.experimental import pallas as pl
from jax.experimental.pallas import tpu as pltpu
from jax.sharding import PartitionSpec as P

FREQS = 16384
LANES = 128
TURN = 0.25 / (2.0 * math.pi)
SIN_TERMS = (4.44286798219978, -7.307445410802044, 3.594802081647382, -0.7844035671777289)
COS_TERMS = (1.414204080722155, -6.977642062283957, 5.715238417642065, -1.728348665863172)
F32 = jnp.float32
BF16 = jnp.bfloat16
MESH = pl.DeviceIdType.MESH


def scaled_trig(turns, amplitude):
    r = turns - jnp.round(turns)
    u = r * r
    half_sin = SIN_TERMS[-1]
    for term in SIN_TERMS[-2::-1]:
        half_sin = half_sin * u + term
    half_sin = half_sin * r
    half_cos = COS_TERMS[-1]
    for term in COS_TERMS[-2::-1]:
        half_cos = half_cos * u + term
    scaled = amplitude * half_sin
    return amplitude - scaled * half_sin, scaled * half_cos


def three_way(value):
    high = value.astype(BF16).astype(F32)
    middle = (value - high).astype(BF16).astype(F32)
    return high, middle, value - high - middle


def lane_fold(value):
    total = value[:, :LANES]
    for start in range(LANES, value.shape[1], LANES):
        total = total + value[:, start : start + LANES]
    return total


def rows_to_lanes(parts):
    stacked = jnp.concatenate(parts, axis=0)
    rest = LANES - stacked.shape[0]
    stacked = jnp.concatenate([stacked, jnp.zeros((rest, LANES), F32)], axis=0)
    return jnp.sum(stacked.T, axis=0, keepdims=True)


def lanes_to_rows(row, offset, count):
    shape = (count, LANES)
    here = lax.broadcasted_iota(jnp.int32, shape, 0) + offset
    lane = lax.broadcasted_iota(jnp.int32, shape, 1)
    picked = jnp.where(here == lane, jnp.broadcast_to(row, shape), jnp.zeros(shape, F32))
    return jnp.sum(picked, axis=1, keepdims=True)


def kernel(
    sizes, points, freq, density, targets, probes, x_out, r_out,
    table, turns_t, rhs, lhs, acc,
    c_part, c_send, c_recv, c_own, c_all, s_send, s_recv, d_all,
    i_part, i_own, i_send, i_recv, i_all, j_send, j_recv, j_all, g_all, h_all,
    a_src, b_src, c_src, d_src, e_src, f_src, z_send, cz_recv, sz_recv,
    e_sums, ex_sums, e_sums_x, ez_sums, e_all, n_sums, nx_sums, n_sums_x, nz_sums, n_all, send_sem, recv_sem, gather_sem,
):
    rows, feats = sizes
    me_r = lax.axis_index("rows")
    me_f = lax.axis_index("feat")
    here = points.shape[1]
    width = freq.shape[1]
    sides = rhs.shape[0]
    share = here // feats
    blocks = block_count(rows)
    members = rows // blocks
    span = width // blocks
    batch = min(1024, here)
    my_member = me_r // blocks
    my_block = lax.rem(me_r, blocks)
    my_place = my_block * members + my_member

    barrier = pltpu.get_barrier_semaphore()

    def greet_row(step, carry):
        pl.semaphore_signal(
            barrier, inc=1, device_id=(lax.rem(me_r + step, rows), me_f), device_id_type=MESH
        )
        return carry

    def greet_feat(step, carry):
        pl.semaphore_signal(
            barrier, inc=1, device_id=(me_r, lax.rem(me_f + step, feats)), device_id_type=MESH
        )
        return carry

    lax.fori_loop(1, rows, greet_row, 0)
    lax.fori_loop(1, feats, greet_feat, 0)

    def across(phase, arrival, src, dst, step):
        target = my_member * blocks + lax.rem(my_block + step, blocks)
        return pltpu.make_async_remote_copy(
            src_ref=src, dst_ref=dst, send_sem=send_sem.at[phase], recv_sem=arrival,
            device_id=(target, me_f), device_id_type=MESH,
        )

    def along(phase, arrival, src, dst, step):
        target = lax.rem(my_member + step, members) * blocks + my_block
        return pltpu.make_async_remote_copy(
            src_ref=src, dst_ref=dst, send_sem=send_sem.at[phase], recv_sem=arrival,
            device_id=(target, me_f), device_id_type=MESH,
        )

    def to_feat(phase, src, dst, step):
        return pltpu.make_async_remote_copy(
            src_ref=src, dst_ref=dst, send_sem=send_sem.at[phase], recv_sem=recv_sem.at[phase],
            device_id=(me_r, lax.rem(me_f + step, feats)), device_id_type=MESH,
        )

    def await_bytes(sem, ref):
        pltpu.make_async_copy(ref, ref, sem).wait()

    rhs[0:1, :] = targets[...]
    rhs[1:sides, :] = (2 * probes[...] - 1).astype(F32)
    right = rhs[...]
    lhs[...] = right.astype(BF16)
    high, middle, low = three_way(points[...] * TURN)
    stacked = jnp.concatenate([high, middle, low, jnp.zeros_like(high)], axis=0)
    turns_t[...] = stacked.T.astype(BF16)
    e_sums[0] = rows_to_lanes([lane_fold(right * right)])

    def make_block(block):
        at = block * span
        whole = freq[:, at : at + span].astype(F32)
        whole = jnp.concatenate([whole, whole, whole, jnp.zeros_like(whole)], axis=0).astype(BF16)
        strength = jnp.exp(0.5 * density[:, at : at + span]) * (1.0 / math.sqrt(FREQS))

        def fill(step, carry):
            first = pl.multiple_of(step * batch, batch)
            turns = jnp.dot(turns_t[pl.ds(first, batch), :], whole, preferred_element_type=F32)
            cosine, sine = scaled_trig(turns, strength)
            table[pl.ds(first, batch), 2 * at : 2 * at + span] = cosine.astype(BF16)
            table[pl.ds(first, batch), 2 * at + span : 2 * (at + span)] = sine.astype(BF16)
            return carry

        lax.fori_loop(0, here // batch, fill, 0)

    def project(block, buffer):
        for part in range(2):
            at = (2 * block + part) * span
            sums = jnp.dot(lhs[...], table[:, at : at + span], preferred_element_type=F32)
            for piece in range(span // LANES):
                member = part * (members // 2) + piece
                value = sums[:, piece * LANES : (piece + 1) * LANES]
                buffer[block * members + member] = value.astype(BF16)

                @pl.when(my_block == block)
                def _():
                    c_part[member] = value

    def ship(block, kit):
        step = lax.rem(block + blocks - my_block, blocks)

        @pl.when(step != 0)
        def _():
            phase = kit.phase
            source = kit.send.at[pl.ds(block * members, members)]
            across(phase, recv_sem.at[phase], source, kit.x_recv.at[step - 1], step).start()
            sums = kit.x_sums.at[pl.ds(step - 1, 1)]
            across(phase + 1, recv_sem.at[phase + 1], kit.sums, sums, step).start()

    def stage_two(block, kit):
        @pl.when(my_block == block)
        def _():
            phase = kit.phase
            await_bytes(recv_sem.at[phase], kit.x_recv)
            await_bytes(recv_sem.at[phase + 1], kit.x_sums)
            total = kit.sums[0]
            for slot in range(blocks - 1):
                total = total + kit.x_sums[slot]
            kit.sums_x[0] = total

            def add(member, carry):
                value = c_part[member]
                for slot in range(blocks - 1):
                    value = value + kit.x_recv[slot, member].astype(F32)
                z_send[member] = value
                return carry

            lax.fori_loop(0, members, add, 0)

            def send(step, carry):
                source = z_send.at[lax.rem(my_member + step, members)]
                along(phase + 2, recv_sem.at[phase + 2], source, kit.z_recv.at[step - 1], step).start()
                sums = kit.z_sums.at[pl.ds(step - 1, 1)]
                along(phase + 3, recv_sem.at[phase + 3], kit.sums_x, sums, step).start()
                return carry

            lax.fori_loop(1, members, send, 0)

    def stage_three(block, kit, finish):
        @pl.when(my_block == block)
        def _():
            phase = kit.phase
            await_bytes(recv_sem.at[phase + 2], kit.z_recv)
            await_bytes(recv_sem.at[phase + 3], kit.z_sums)
            sums = kit.sums_x[0]
            for slot in range(members - 1):
                sums = sums + kit.z_sums[slot]
            kit.sums_all[...] = sums
            total = z_send[my_member]
            for slot in range(members - 1):
                total = total + kit.z_recv[slot]
            value = finish(total, sums).astype(BF16)
            kit.source[...] = value
            kit.everyone[my_place] = value

            def send(step, carry):
                target = kit.everyone.at[my_place]
                along(phase + 4, recv_sem.at[phase + 4], kit.source, target, step).start()
                return carry

            lax.fori_loop(1, members, send, 0)
            await_bytes(send_sem.at[phase + 2], kit.z_recv)

    def stage_four(block, kit):
        @pl.when(my_block == block)
        def _():
            phase = kit.phase
            await_bytes(recv_sem.at[phase + 4], kit.everyone.at[pl.ds(0, members - 1)])
            whole = kit.everyone.at[pl.ds(block * members, members)]

            def send(step, carry):
                across(phase + 5, gather_sem.at[kit.turn, block], whole, whole, step).start()
                return carry

            lax.fori_loop(1, blocks, send, 0)

    def await_block(block, kit):
        @pl.when(my_block != block)
        def _():
            region = kit.everyone.at[pl.ds(block * members, members)]
            await_bytes(gather_sem.at[kit.turn, block], region)

    def finish_rows(kit):
        phase = kit.phase
        await_bytes(send_sem.at[phase], kit.x_recv)
        await_bytes(send_sem.at[phase + 1], kit.x_sums)
        await_bytes(send_sem.at[phase + 3], kit.z_sums)
        await_bytes(send_sem.at[phase + 4], kit.everyone.at[pl.ds(0, members - 1)])
        await_bytes(send_sem.at[phase + 5], kit.everyone.at[pl.ds(0, (blocks - 1) * members)])

    def gathered(everyone, first, last):
        places = range(first * members, last * members)
        return jnp.concatenate([everyone[place] for place in places], axis=1)

    def raise_block(block, everyone, half):
        left = gathered(everyone, block, block + 1)
        slab = min(1024, here // 2)
        count = here // slab // 2

        def one(step, carry):
            at = pl.multiple_of(step * slab, slab)
            part = lax.dot_general(
                left, table[pl.ds(at, slab), 2 * block * span : 2 * (block + 1) * span],
                (((1,), (1,)), ((), ())), preferred_element_type=F32,
            )
            acc[:, pl.ds(at, slab)] = part if block == 0 else acc[:, pl.ds(at, slab)] + part
            return carry

        lax.fori_loop(half * count, (half + 1) * count, one, 0)

    def raise_rest(phase, early, everyone, buffer, landing, norms, norm_src):
        wide = gathered(everyone, 0, blocks).astype(F32)
        norm_src[...] = jnp.broadcast_to(rows_to_lanes([lane_fold(wide * wide)]), (8, LANES))
        norms[me_f] = norm_src[...]

        def send(step, carry):
            to_feat(phase + 6, norm_src, norms.at[me_f], step).start()
            return carry

        lax.fori_loop(1, feats, send, 0)

        def one(index, carry):
            step = index + 1
            target = lax.rem(me_f + step, feats)
            at = pl.multiple_of(target * share, share)
            images = acc[:, pl.ds(at, share)] + lax.dot_general(
                gathered(everyone, early, blocks),
                table[pl.ds(at, share), 2 * early * span : 2 * width],
                (((1,), (1,)), ((), ())), preferred_element_type=F32,
            )
            buffer[target] = images

            @pl.when(step < feats)
            def _():
                to_feat(phase, buffer.at[target], landing.at[step - 1], step).start()

            @pl.when(step == feats)
            def _():
                i_part[...] = images

            return carry

        lax.fori_loop(0, feats, one, 0)
        await_bytes(recv_sem.at[phase + 6], norms.at[pl.ds(0, feats - 1)])
        squares = norms[0, 0:1, :]
        for part in range(1, feats):
            squares = squares + norms[part, 0:1, :]
        await_bytes(recv_sem.at[phase], landing)
        total = i_part[...]
        for slot in range(feats - 1):
            total = total + landing[slot]
        return total, lanes_to_rows(squares, 0, sides)

    def share_feats(phase, source, everyone, value):
        source[...] = value
        everyone[me_f] = value

        def send(step, carry):
            to_feat(phase, source, everyone.at[me_f], step).start()
            return carry

        lax.fori_loop(1, feats, send, 0)

    def await_feats(phase, everyone):
        await_bytes(recv_sem.at[phase], everyone.at[pl.ds(0, feats - 1)])
        return jnp.concatenate([everyone[part] for part in range(feats)], axis=1)

    early = blocks - 1
    one_kit = SimpleNamespace(
        phase=16, turn=0, send=c_send, x_recv=c_recv, z_recv=cz_recv, everyone=c_all, source=a_src,
        sums=e_sums, x_sums=ex_sums, sums_x=e_sums_x, z_sums=ez_sums, sums_all=e_all,
    )
    two_kit = SimpleNamespace(
        phase=22, turn=1, send=s_send, x_recv=s_recv, z_recv=sz_recv, everyone=d_all, source=c_src,
        sums=n_sums, x_sums=nx_sums, sums_x=n_sums_x, z_sums=nz_sums, sums_all=n_all,
    )

    def keep_first(total, sums):
        c_own[...] = total
        return total

    kit = one_kit
    make_block(0)
    project(0, c_send)
    make_block(1)
    pl.semaphore_wait(barrier, rows + feats - 2)
    ship(0, kit)
    project(1, c_send)
    ship(1, kit)
    make_block(2)
    stage_two(0, kit)
    project(2, c_send)
    ship(2, kit)
    stage_three(0, kit, keep_first)
    stage_two(1, kit)
    make_block(3)
    stage_four(0, kit)
    stage_three(1, kit, keep_first)
    stage_two(2, kit)
    project(3, c_send)
    ship(3, kit)
    stage_four(1, kit)
    stage_three(2, kit, keep_first)
    await_block(0, kit)
    raise_block(0, c_all, 0)
    raise_block(0, c_all, 1)
    stage_four(2, kit)
    stage_two(3, kit)
    await_block(1, kit)
    raise_block(1, c_all, 0)
    raise_block(1, c_all, 1)
    stage_three(3, kit, keep_first)
    await_block(2, kit)
    raise_block(2, c_all, 0)
    stage_four(3, kit)
    raise_block(2, c_all, 1)
    await_block(3, kit)
    total, squares = raise_rest(2, early, c_all, i_send, i_recv, g_all, e_src)
    i_own[...] = total
    share_feats(3, b_src, i_all, total.astype(BF16))
    energy = lanes_to_rows(e_all[...], 0, sides)
    alpha0 = energy / (squares + energy)
    images = await_feats(3, i_all)
    lhs[...] = images
    residual = (1.0 - alpha0) * rhs[...] - alpha0 * images.astype(F32)
    n_sums[0] = rows_to_lanes([lane_fold(residual * residual), lane_fold(residual * rhs[...])])

    def combine(total, sums):
        beta = lanes_to_rows(sums, 0, sides) / energy
        return (1.0 - alpha0 + beta) * c_own[...] - alpha0 * total

    kit = two_kit
    project(0, s_send)
    ship(0, kit)
    project(1, s_send)
    ship(1, kit)
    stage_two(0, kit)
    project(2, s_send)
    ship(2, kit)
    stage_three(0, kit, combine)
    stage_two(1, kit)
    project(3, s_send)
    ship(3, kit)
    stage_four(0, kit)
    stage_three(1, kit, combine)
    stage_two(2, kit)
    await_block(0, kit)
    raise_block(0, d_all, 0)
    stage_four(1, kit)
    stage_three(2, kit, combine)
    raise_block(0, d_all, 1)
    stage_two(3, kit)
    await_block(1, kit)
    raise_block(1, d_all, 0)
    stage_four(2, kit)
    raise_block(1, d_all, 1)
    stage_three(3, kit, combine)
    await_block(2, kit)
    raise_block(2, d_all, 0)
    stage_four(3, kit)
    raise_block(2, d_all, 1)
    await_block(3, kit)
    total, squares = raise_rest(6, early, d_all, j_send, j_recv, h_all, f_src)
    energy_next = lanes_to_rows(n_all[...], 0, sides)
    cross = lanes_to_rows(n_all[...], sides, sides)
    beta = energy_next / energy
    direction_energy = energy_next + beta * (2.0 * cross + beta * energy)
    alpha1 = energy_next / (squares + direction_energy)

    mine = rhs[:, pl.ds(pl.multiple_of(me_f * share, share), share)]
    residual = (1.0 - alpha0) * mine - alpha0 * i_own[...]
    residual = residual - alpha1 * (total + residual + beta * mine)
    share_feats(7, d_src, j_all, residual.astype(BF16))
    right = rhs[...]
    residual = (1.0 - alpha0) * right - alpha0 * lhs[...].astype(F32)
    x_out[...] = alpha0 * right + alpha1 * (residual + beta * right)
    r_out[...] = await_feats(7, j_all).astype(F32)

    for phase, ref in (
        (2, i_recv), (3, i_all.at[pl.ds(0, feats - 1)]),
        (6, j_recv), (7, j_all.at[pl.ds(0, feats - 1)]),
        (8, g_all.at[pl.ds(0, feats - 1)]), (12, h_all.at[pl.ds(0, feats - 1)]),
    ):
        await_bytes(send_sem.at[phase], ref)
    finish_rows(one_kit)
    finish_rows(two_kit)


def block_count(rows):
    return 4


def local(sizes, points, freq_index, log_density, targets, probes):
    rows, feats = sizes
    here = points.shape[1]
    width = freq_index.shape[1]
    sides = probes.shape[0] + 1
    share = here // feats
    vmem = pl.BlockSpec(memory_space=pltpu.VMEM)
    out = jax.ShapeDtypeStruct((sides, here), F32)
    block = (sides, LANES)
    blocks = block_count(rows)
    members = rows // blocks
    scratch = [
        pltpu.VMEM((here, 2 * width), BF16),
        pltpu.VMEM((here, 32), BF16),
        pltpu.VMEM((sides, here), F32),
        pltpu.VMEM((sides, here), BF16),
        pltpu.VMEM((sides, here), F32),
        pltpu.VMEM((members, *block), F32),
        pltpu.VMEM((rows, *block), BF16),
        pltpu.VMEM((blocks - 1, members, *block), BF16),
        pltpu.VMEM((sides, LANES), F32),
        pltpu.VMEM((rows, sides, LANES), BF16),
        pltpu.VMEM((rows, *block), BF16),
        pltpu.VMEM((blocks - 1, members, *block), BF16),
        pltpu.VMEM((rows, sides, LANES), BF16),
        pltpu.VMEM((sides, share), F32),
        pltpu.VMEM((sides, share), F32),
        pltpu.VMEM((feats, sides, share), F32),
        pltpu.VMEM((feats - 1, sides, share), F32),
        pltpu.VMEM((feats, sides, share), BF16),
        pltpu.VMEM((feats, sides, share), F32),
        pltpu.VMEM((feats - 1, sides, share), F32),
        pltpu.VMEM((feats, sides, share), BF16),
        pltpu.VMEM((feats, 8, LANES), F32),
        pltpu.VMEM((feats, 8, LANES), F32),
        pltpu.VMEM((sides, LANES), BF16),
        pltpu.VMEM((sides, share), BF16),
        pltpu.VMEM((sides, LANES), BF16),
        pltpu.VMEM((sides, share), BF16),
        pltpu.VMEM((8, LANES), F32),
        pltpu.VMEM((8, LANES), F32),
        pltpu.VMEM((members, *block), F32),
        pltpu.VMEM((members - 1, *block), F32),
        pltpu.VMEM((members - 1, *block), F32),
    ] + 2 * [
        pltpu.VMEM((1, 1, LANES), F32),
        pltpu.VMEM((blocks - 1, 1, LANES), F32),
        pltpu.VMEM((1, 1, LANES), F32),
        pltpu.VMEM((members - 1, 1, LANES), F32),
        pltpu.VMEM((1, LANES), F32),
    ] + [
        pltpu.SemaphoreType.DMA((28,)),
        pltpu.SemaphoreType.DMA((28,)),
        pltpu.SemaphoreType.DMA((2, block_count(rows))),
    ]
    return pl.pallas_call(
        functools.partial(kernel, sizes),
        out_shape=(out, out),
        in_specs=[vmem] * 5,
        out_specs=(vmem, vmem),
        scratch_shapes=scratch,
        name="regress",
        compiler_params=pltpu.CompilerParams(
            collective_id=0, has_side_effects=True, vmem_limit_bytes=56 << 20
        ),
    )(points, freq_index, log_density.reshape(1, width), targets.reshape(1, here), probes)


def solution(mesh):
    sizes = (mesh.shape["rows"], mesh.shape["feat"])
    in_specs = (P(None, "rows"), P(None, "feat"), P("feat"), P("rows"), P(None, "rows"))
    out_specs = (P(None, "rows"), P(None, "rows"))
    return jax.shard_map(
        functools.partial(local, sizes),
        mesh=mesh, in_specs=in_specs, out_specs=out_specs, check_vma=False,
    )
```

```python
import functools
import math

import jax
import jax.numpy as jnp
from jax import lax
from jax.experimental import pallas as pl
from jax.experimental.pallas import tpu as pltpu
from jax.sharding import PartitionSpec as P

FREQS = 16384
LANES = 128
TURN = 0.25 / (2.0 * math.pi)
SIN_TERMS = (4.44286798219978, -7.307445410802044, 3.594802081647382, -0.7844035671777289)
COS_TERMS = (1.414204080722155, -6.977642062283957, 5.715238417642065, -1.728348665863172)
F32 = jnp.float32
BF16 = jnp.bfloat16
MESH = pl.DeviceIdType.MESH


def scaled_trig(turns, amplitude):
    r = turns - jnp.round(turns)
    u = r * r
    half_sin = SIN_TERMS[-1]
    for term in SIN_TERMS[-2::-1]:
        half_sin = half_sin * u + term
    half_sin = half_sin * r
    half_cos = COS_TERMS[-1]
    for term in COS_TERMS[-2::-1]:
        half_cos = half_cos * u + term
    scaled = amplitude * half_sin
    return amplitude - scaled * half_sin, scaled * half_cos


def three_way(value):
    high = value.astype(BF16).astype(F32)
    middle = (value - high).astype(BF16).astype(F32)
    return high, middle, value - high - middle


def spread(value, axis, shape):
    high, middle, low = three_way(value)
    place = lax.broadcasted_iota(jnp.int32, shape, axis)
    high, middle, low = (jnp.broadcast_to(part, shape) for part in (high, middle, low))
    zero = jnp.zeros(shape, F32)
    return jnp.where(
        place == 0, high, jnp.where(place == 1, middle, jnp.where(place == 2, low, zero))
    )


def lane_fold(value):
    total = value[:, :LANES]
    for start in range(LANES, value.shape[1], LANES):
        total = total + value[:, start : start + LANES]
    return total


def rows_to_lanes(parts):
    stacked = jnp.concatenate(parts, axis=0)
    rest = LANES - stacked.shape[0]
    stacked = jnp.concatenate([stacked, jnp.zeros((rest, LANES), F32)], axis=0)
    return jnp.sum(stacked.T, axis=0, keepdims=True)


def lanes_to_rows(row, offset, count):
    shape = (count, LANES)
    here = lax.broadcasted_iota(jnp.int32, shape, 0) + offset
    lane = lax.broadcasted_iota(jnp.int32, shape, 1)
    picked = jnp.where(here == lane, jnp.broadcast_to(row, shape), jnp.zeros(shape, F32))
    return jnp.sum(picked, axis=1, keepdims=True)


def kernel(
    sizes, points, freq, density, targets, probes, x_out, r_out,
    table, turns_t, rhs, lhs, acc,
    c_part, c_send, c_recv, c_own, c_all, s_send, s_recv, d_all,
    i_part, i_own, i_send, i_recv, i_all, j_send, j_recv, j_all, g_all, h_all,
    a_src, b_src, c_src, d_src, e_src, f_src, send_sem, recv_sem, gather_sem,
):
    rows, feats = sizes
    me_r = lax.axis_index("rows")
    me_f = lax.axis_index("feat")
    here = points.shape[1]
    width = freq.shape[1]
    sides = rhs.shape[0]
    share = here // feats
    blocks = block_count(rows)
    members = rows // blocks
    span = width // blocks
    batch = min(2048, here)
    sub = max(LANES, span // 2)
    my_member = me_r // blocks
    my_block = lax.rem(me_r + my_member, blocks)
    my_place = my_block * members + my_member

    def owner(block, member):
        return member * blocks + lax.rem(block + members * blocks - member, blocks)


    barrier = pltpu.get_barrier_semaphore()

    def greet_row(step, carry):
        pl.semaphore_signal(
            barrier, inc=1, device_id=(lax.rem(me_r + step, rows), me_f), device_id_type=MESH
        )
        return carry

    def greet_feat(step, carry):
        pl.semaphore_signal(
            barrier, inc=1, device_id=(me_r, lax.rem(me_f + step, feats)), device_id_type=MESH
        )
        return carry

    lax.fori_loop(1, rows, greet_row, 0)
    lax.fori_loop(1, feats, greet_feat, 0)

    def to_row(phase, arrival, src, dst, step):
        return pltpu.make_async_remote_copy(
            src_ref=src, dst_ref=dst, send_sem=send_sem.at[phase], recv_sem=arrival,
            device_id=(lax.rem(me_r + step, rows), me_f), device_id_type=MESH,
        )

    def to_feat(phase, src, dst, step):
        return pltpu.make_async_remote_copy(
            src_ref=src, dst_ref=dst, send_sem=send_sem.at[phase], recv_sem=recv_sem.at[phase],
            device_id=(me_r, lax.rem(me_f + step, feats)), device_id_type=MESH,
        )

    def await_bytes(sem, ref):
        pltpu.make_async_copy(ref, ref, sem).wait()

    rhs[0:1, :] = targets[...]
    rhs[1:sides, :] = (2 * probes[...] - 1).astype(F32)
    right = rhs[...]
    lhs[...] = right.astype(BF16)
    high, middle, low = three_way(points[...] * TURN)
    stacked = jnp.concatenate([high, middle, low, jnp.zeros_like(high)], axis=0)
    turns_t[...] = stacked.T.astype(BF16)
    tail = spread(rows_to_lanes([lane_fold(right * right)]), 0, (16, LANES)).astype(BF16)

    def set_tail(buffer, tail):
        def put(chunk, carry):
            buffer[chunk, sides : sides + 16, :] = tail
            return carry

        lax.fori_loop(0, rows, put, 0)

    set_tail(c_send, tail)

    def make_block(block):
        at = block * span
        whole = freq[:, at : at + span].astype(F32)
        whole = jnp.concatenate([whole, whole, whole, jnp.zeros_like(whole)], axis=0).astype(BF16)
        strength = jnp.exp(0.5 * density[:, at : at + span]) * (1.0 / math.sqrt(FREQS))

        acc[:, 2 * at : 2 * (at + span)] = jnp.zeros((sides, 2 * span), F32)

        def fill(step, carry):
            first = pl.multiple_of(step * batch, batch)
            here_turns = turns_t[pl.ds(first, batch), :]
            left = lhs[:, pl.ds(first, batch)]

            def add(values, start):
                acc[:, start : start + sub] += jnp.dot(left, values, preferred_element_type=F32)

            pending = []
            turns = jnp.dot(here_turns, whole[:, 0:sub], preferred_element_type=F32)
            for start in range(0, span, sub):
                later = start + sub
                ahead = turns
                if later < span:
                    ahead = jnp.dot(
                        here_turns, whole[:, later : later + sub], preferred_element_type=F32
                    )
                cosine, sine = scaled_trig(turns, strength[:, start : start + sub])
                cosine = cosine.astype(BF16)
                sine = sine.astype(BF16)
                for values, place in pending:
                    add(values, place)
                table[pl.ds(first, batch), 2 * at + start : 2 * at + start + sub] = cosine
                shifted = 2 * at + span + start
                table[pl.ds(first, batch), shifted : shifted + sub] = sine
                pending = [(cosine, 2 * at + start), (sine, shifted)]
                turns = ahead
            for values, place in pending:
                add(values, place)
            return carry

        lax.fori_loop(0, here // batch, fill, 0)

    def project(block, buffer, known=False):
        for part in range(2):
            at = (2 * block + part) * span
            if known:
                sums = acc[:, at : at + span]
            else:
                sums = acc[:, at : at + span]
                for other in range(1, feats // 2):
                    which = lax.rem(me_f // 2 + other, feats // 2)
                    left = jnp.concatenate([i_all[2 * which], i_all[2 * which + 1]], axis=1)
                    first = pl.multiple_of(which * (2 * share), 2 * share)
                    sums = sums + jnp.dot(
                        left, table[pl.ds(first, 2 * share), at : at + span],
                        preferred_element_type=F32,
                    )
            for piece in range(span // LANES):
                member = part * (members // 2) + piece
                value = sums[:, piece * LANES : (piece + 1) * LANES]
                buffer[block * members + member, 0:sides, :] = value.astype(BF16)

                @pl.when(my_place == block * members + member)
                def _():
                    c_part[...] = value

    def ship(phase, block, buffer, landing):
        def send(member, carry):
            step = lax.rem(owner(block, member) + rows - me_r, rows)

            @pl.when(step != 0)
            def _():
                to_row(
                    phase, recv_sem.at[phase], buffer.at[block * members + member],
                    landing.at[step - 1], step,
                ).start()

            return carry

        lax.fori_loop(0, members, send, 0)

    def collect(phase, landing, buffer):
        await_bytes(recv_sem.at[phase], landing)

        def add(slot, carry):
            total, extra = carry
            total = total + landing[slot, 0:sides, :].astype(F32)
            return total, extra + landing[slot, sides : sides + 16, :].astype(F32)

        first = (c_part[...], buffer[0, sides : sides + 16, :].astype(F32))
        total, extra = lax.fori_loop(0, rows - 1, add, first)
        return total, jnp.sum(extra, axis=0, keepdims=True)

    def share_rows(phase, block, source, everyone, value):
        source[...] = value
        everyone[my_place] = value

        def send(step, carry):
            arrival = gather_sem.at[phase // 4, block]
            to_row(phase, arrival, source, everyone.at[my_place], step).start()
            return carry

        lax.fori_loop(1, rows, send, 0)

    def await_block(phase, block, everyone):
        arrival = gather_sem.at[phase // 4, block]

        @pl.when(my_block == block)
        def _():
            await_bytes(arrival, everyone.at[pl.ds(block * members, members - 1)])

        @pl.when(my_block != block)
        def _():
            await_bytes(arrival, everyone.at[pl.ds(block * members, members)])

    def gathered(everyone, first, last):
        places = range(first * members, last * members)
        return jnp.concatenate([everyone[place] for place in places], axis=1)

    def raise_block(block, everyone, half):
        left = gathered(everyone, block, block + 1)
        slab = min(1024, here // 2)
        count = here // slab // 2

        def one(step, carry):
            at = pl.multiple_of(step * slab, slab)
            part = lax.dot_general(
                left, table[pl.ds(at, slab), 2 * block * span : 2 * (block + 1) * span],
                (((1,), (1,)), ((), ())), preferred_element_type=F32,
            )
            acc[:, pl.ds(at, slab)] = part if block == 0 else acc[:, pl.ds(at, slab)] + part
            return carry

        lax.fori_loop(half * count, (half + 1) * count, one, 0)

    def raise_rest(phase, early, everyone, buffer, landing, norms, norm_src):
        wide = gathered(everyone, 0, blocks).astype(F32)
        norm_src[...] = jnp.broadcast_to(rows_to_lanes([lane_fold(wide * wide)]), (8, LANES))
        norms[me_f] = norm_src[...]

        def send(step, carry):
            to_feat(phase + 6, norm_src, norms.at[me_f], step).start()
            return carry

        lax.fori_loop(1, feats, send, 0)

        def one(index, carry):
            pair = lax.rem(me_f // 2 + index // 2 + 1, feats // 2)
            target = 2 * pair + lax.rem(me_f + 1 + index, 2)
            step = lax.rem(target + feats - me_f, feats)
            at = pl.multiple_of(target * share, share)
            images = acc[:, pl.ds(at, share)] + lax.dot_general(
                gathered(everyone, early, blocks),
                table[pl.ds(at, share), 2 * early * span : 2 * width],
                (((1,), (1,)), ((), ())), preferred_element_type=F32,
            )
            buffer[target] = images

            @pl.when(step != 0)
            def _():
                to_feat(phase, buffer.at[target], landing.at[step - 1], step).start()

            @pl.when(step == 0)
            def _():
                i_part[...] = images

            return carry

        lax.fori_loop(0, feats, one, 0)
        await_bytes(recv_sem.at[phase + 6], norms.at[pl.ds(0, feats - 1)])
        squares = norms[0, 0:1, :]
        for part in range(1, feats):
            squares = squares + norms[part, 0:1, :]
        await_bytes(recv_sem.at[phase], landing)
        total = i_part[...]
        for slot in range(feats - 1):
            total = total + landing[slot]
        return total, lanes_to_rows(squares, 0, sides)

    def share_feats(phase, source, everyone, value):
        source[...] = value
        everyone[me_f] = value

        def send(step, carry):
            to_feat(phase, source, everyone.at[me_f], step).start()
            return carry

        lax.fori_loop(1, feats, send, 0)

    def await_feats(phase, everyone):
        await_bytes(recv_sem.at[phase], everyone.at[pl.ds(0, feats - 1)])
        return jnp.concatenate([everyone[part] for part in range(feats)], axis=1)

    early = max(1, blocks - 2)

    def own_first(block):
        @pl.when(my_block == block)
        def _():
            total, extra = collect(0, c_recv, c_send)
            c_own[0:sides, :] = total
            c_own[sides : sides + 8, :] = jnp.broadcast_to(extra, (8, LANES))
            share_rows(1, block, a_src, c_all, total.astype(BF16))

    make_block(0)
    project(0, c_send, True)
    make_block(1)
    pl.semaphore_wait(barrier, rows + feats - 2)
    ship(0, 0, c_send, c_recv)
    project(1, c_send, True)
    ship(0, 1, c_send, c_recv)
    for block in range(2, blocks):
        make_block(block)
        project(block, c_send, True)
        ship(0, block, c_send, c_recv)
        own_first(block - 2)
    own_first(blocks - 2)
    for block in range(early):
        await_block(0, block, c_all)
        raise_block(block, c_all, 0)
        if block == 0:
            own_first(blocks - 1)
        raise_block(block, c_all, 1)
    for block in range(early, blocks):
        await_block(0, block, c_all)
    total, squares = raise_rest(2, early, c_all, i_send, i_recv, g_all, e_src)
    i_own[...] = total
    b_src[...] = total.astype(BF16)
    i_all[me_f] = b_src[...]
    chip = me_f // 2
    to_sibling = lax.rem(2 * chip + lax.rem(me_f + 1, 2) + feats - me_f, feats)

    def send_far(step, carry):
        @pl.when(step != to_sibling)
        def _():
            to_feat(3, b_src, i_all.at[me_f], step).start()

        return carry

    lax.fori_loop(1, feats, send_far, 0)
    to_feat(11, b_src, i_all.at[me_f], to_sibling).start()
    energy = lanes_to_rows(c_own[sides : sides + 1, :], 0, sides)
    alpha0 = energy / (squares + energy)
    await_bytes(recv_sem.at[11], i_all.at[pl.ds(0, 1)])

    def pair_of(which):
        return jnp.concatenate([i_all[2 * which], i_all[2 * which + 1]], axis=1)

    def rows_of(which):
        return pl.ds(pl.multiple_of(which * (2 * share), 2 * share), 2 * share)

    near = pair_of(chip)
    for part in range(2 * blocks):
        at = part * span
        acc[:, at : at + span] = jnp.dot(
            near, table[rows_of(chip), at : at + span], preferred_element_type=F32
        )
    if feats > 2:
        await_bytes(recv_sem.at[3], i_all.at[pl.ds(0, feats - 2)])
    images = jnp.concatenate([i_all[part] for part in range(feats)], axis=1)
    lhs[...] = images
    residual = (1.0 - alpha0) * rhs[...] - alpha0 * images.astype(F32)
    tail = rows_to_lanes([lane_fold(residual * residual), lane_fold(residual * rhs[...])])
    set_tail(s_send, spread(tail, 0, (16, LANES)).astype(BF16))

    def own_second(block):
        @pl.when(my_block == block)
        def _():
            total, extra = collect(4, s_recv, s_send)
            beta = lanes_to_rows(extra, 0, sides) / energy
            total = (1.0 - alpha0 + beta) * c_own[0:sides, :] - alpha0 * total
            c_own[sides : sides + 8, :] = jnp.broadcast_to(extra, (8, LANES))
            share_rows(5, block, c_src, d_all, total.astype(BF16))

    for block in range(blocks):
        project(block, s_send)
        ship(4, block, s_send, s_recv)
        if block >= 2:
            own_second(block - 2)
    if blocks == 2:
        own_second(0)
    for block in range(early):
        await_block(4, block, d_all)
        if block == 0 and blocks > 2:
            own_second(blocks - 2)
        raise_block(block, d_all, 0)
        if block == 0:
            own_second(blocks - 1)
        raise_block(block, d_all, 1)
    for block in range(early, blocks):
        await_block(4, block, d_all)
    total, squares = raise_rest(6, early, d_all, j_send, j_recv, h_all, f_src)
    energy_next = lanes_to_rows(c_own[sides : sides + 1, :], 0, sides)
    cross = lanes_to_rows(c_own[sides : sides + 1, :], sides, sides)
    beta = energy_next / energy
    direction_energy = energy_next + beta * (2.0 * cross + beta * energy)
    alpha1 = energy_next / (squares + direction_energy)

    mine = rhs[:, pl.ds(pl.multiple_of(me_f * share, share), share)]
    residual = (1.0 - alpha0) * mine - alpha0 * i_own[...]
    residual = residual - alpha1 * (total + residual + beta * mine)
    share_feats(7, d_src, j_all, residual.astype(BF16))
    right = rhs[...]
    residual = (1.0 - alpha0) * right - alpha0 * lhs[...].astype(F32)
    x_out[...] = alpha0 * right + alpha1 * (residual + beta * right)
    r_out[...] = await_feats(7, j_all).astype(F32)

    for phase, ref in (
        (0, c_recv), (1, c_all.at[pl.ds(0, rows - 1)]),
        (2, i_recv), (11, i_all.at[pl.ds(0, 1)]),
        (4, s_recv), (5, d_all.at[pl.ds(0, rows - 1)]),
        (6, j_recv), (7, j_all.at[pl.ds(0, feats - 1)]),
        (8, g_all.at[pl.ds(0, feats - 1)]), (12, h_all.at[pl.ds(0, feats - 1)]),
    ):
        await_bytes(send_sem.at[phase], ref)
    if feats > 2:
        await_bytes(send_sem.at[3], i_all.at[pl.ds(0, feats - 2)])


def block_count(rows):
    return 4 if rows % 8 == 0 else 2


def local(sizes, points, freq_index, log_density, targets, probes):
    rows, feats = sizes
    here = points.shape[1]
    width = freq_index.shape[1]
    sides = probes.shape[0] + 1
    share = here // feats
    vmem = pl.BlockSpec(memory_space=pltpu.VMEM)
    out = jax.ShapeDtypeStruct((sides, here), F32)
    block = (sides + 16, LANES)
    scratch = [
        pltpu.VMEM((here, 2 * width), BF16),
        pltpu.VMEM((here, 32), BF16),
        pltpu.VMEM((sides, here), F32),
        pltpu.VMEM((sides, here), BF16),
        pltpu.VMEM((sides, max(here, 2 * width)), F32),
        pltpu.VMEM((sides, LANES), F32),
        pltpu.VMEM((rows, *block), BF16),
        pltpu.VMEM((rows - 1, *block), BF16),
        pltpu.VMEM((sides + 8, LANES), F32),
        pltpu.VMEM((rows, sides, LANES), BF16),
        pltpu.VMEM((rows, *block), BF16),
        pltpu.VMEM((rows - 1, *block), BF16),
        pltpu.VMEM((rows, sides, LANES), BF16),
        pltpu.VMEM((sides, share), F32),
        pltpu.VMEM((sides, share), F32),
        pltpu.VMEM((feats, sides, share), F32),
        pltpu.VMEM((feats - 1, sides, share), F32),
        pltpu.VMEM((feats, sides, share), BF16),
        pltpu.VMEM((feats, sides, share), F32),
        pltpu.VMEM((feats - 1, sides, share), F32),
        pltpu.VMEM((feats, sides, share), BF16),
        pltpu.VMEM((feats, 8, LANES), F32),
        pltpu.VMEM((feats, 8, LANES), F32),
        pltpu.VMEM((sides, LANES), BF16),
        pltpu.VMEM((sides, share), BF16),
        pltpu.VMEM((sides, LANES), BF16),
        pltpu.VMEM((sides, share), BF16),
        pltpu.VMEM((8, LANES), F32),
        pltpu.VMEM((8, LANES), F32),
        pltpu.SemaphoreType.DMA((13,)),
        pltpu.SemaphoreType.DMA((13,)),
        pltpu.SemaphoreType.DMA((2, block_count(rows))),
    ]
    return pl.pallas_call(
        functools.partial(kernel, sizes),
        out_shape=(out, out),
        in_specs=[vmem] * 5,
        out_specs=(vmem, vmem),
        scratch_shapes=scratch,
        name="regress",
        compiler_params=pltpu.CompilerParams(
            collective_id=0, has_side_effects=True, vmem_limit_bytes=56 << 20
        ),
    )(points, freq_index, log_density.reshape(1, width), targets.reshape(1, here), probes)


def solution(mesh):
    sizes = (mesh.shape["rows"], mesh.shape["feat"])
    in_specs = (P(None, "rows"), P(None, "feat"), P("feat"), P("rows"), P(None, "rows"))
    out_specs = (P(None, "rows"), P(None, "rows"))
    return jax.shard_map(
        functools.partial(local, sizes),
        mesh=mesh, in_specs=in_specs, out_specs=out_specs, check_vma=False,
    )
```
